32 devices in a mesh: illum: 2 (over x), box: 16 (over z, y, core).
Axes of the slice: x: 2, y: 2, z: 4, core: 2. Of those that a mesh axis runs over, the one named last changes fastest.
Arguments:
- patterns: bfloat16 [2, 256, 128, 256], P(None, 'box', None, 'illum'), parts along dimension 3, may hold values from -6 to 6
- owner_block: int32 [4], replicated, may hold values from 0 to 31
- low_index: int32 [256, 48], P('box'), may hold values from 0 to 315
- low_mask: int32 [256, 48], P('box'), may hold values 0 or 1
- low_table: bfloat16 [2, 316, 128], replicated, may hold values from -2 to 2
- interp: bfloat16 [128, 512], replicated, may hold values from -0.5 to 0.5
- shift_angle: float32 [8, 512], replicated, may hold values from -3.140625 to 3.140625
- par_source: int32 [32, 16], replicated, may hold values from 0 to 31, as said below
- par_index: int32 [32, 16], replicated, may hold values from 0 to 315
- par_mask: int32 [32, 16], replicated, may hold values 0 or 1
- par_table: bfloat16 [2, 316, 512], replicated, may hold values from -1.5 to 1.5
Outputs:
- incoming: float32 [2, 256, 128, 256], P(None, 'box', None, 'illum'), parts along dimension 3
The draws below stay inside these ranges and needn't reach their ends.
There are 2 independent parts, one for each index of `illum`. The reference program is written for one: setup_inputs(seed, part) draws one part's arguments, and reference() takes and returns one part's arrays. A program takes and returns all parts, laid end to end along the dimension named above; an argument that names none is the same for every part. Nothing has to cross between parts.
Inputs may be any that keep to these rules, and one draw needn't show every extreme that they name: `par_source`: each parent's 16 slots name distinct parents other than itself.
All inputs are finite; a program needn't handle non-finite values. No bound on the sum of `low_mask` on one device may be relied on, other than what follows from the above.
Results may differ from the reference program's by a relative error of at most 0.0047.
Values may be sent and summed in bfloat16 or wider, within the bound.
A program may use at most 64 MiB of HBM per device.

```python
import jax
import jax.numpy as jnp
from jax import lax

K = 128
Q = 512
R = 128
BOX_DEV = 16
STEPS = 4
NTRANS = 316
PLIST = 16
BOXES = 256
BLOCKS = 32
PARENTS = 32
SRC = 48


def draw_par_source(key, part):
    row_keys = jax.random.split(jax.random.fold_in(key, 7), PARENTS)

    def one_row(row_key):
        rest = jax.random.permutation(row_key, PARENTS - 2).astype(jnp.int32) + 2
        return jnp.concatenate([jnp.ones((1,), jnp.int32), rest[:PLIST - 1]])
    offsets = jax.vmap(one_row)(row_keys)
    base = jnp.arange(PARENTS, dtype=jnp.int32)[:, None]
    return ((base + offsets) % PARENTS).astype(jnp.int32)


def place_ends(array, stream_key, least, top_value):
    longest = array.shape.index(max(array.shape))
    spots = []
    for shift in (0, 1):
        where = [jax.random.randint(jax.random.fold_in(stream_key, axis), (), 0, length) for axis, length in enumerate(array.shape)]
        where[longest] = (where[longest] + shift) % array.shape[longest]
        spots.append(tuple(where))
    return array.at[spots[0]].set(least).at[spots[1]].set(top_value)


def block_scale(rng, dims, pieces, smallest, high):
    def one(axis_at, blocks):
        draws = jax.random.uniform(jax.random.fold_in(jax.random.fold_in(rng, 6), axis_at), (blocks,), jnp.float32, smallest / len(pieces), high / len(pieces))
        return jnp.repeat(jnp.exp(draws), dims[axis_at] // blocks).reshape((-1,) + (1,) * (len(dims) - axis_at - 1))

    factor_of = one(*pieces[0])
    for cut in pieces[1:]:
        factor_of = factor_of * one(*cut)
    return factor_of


def gaussian(rng, shape, width, reach, pieces=(), kind=jnp.bfloat16):
    level = block_scale(rng, shape, pieces, -0.22, 0.18) if pieces else 1.0
    values = jax.random.normal(rng, shape, jnp.float32) * width * level
    return jnp.minimum(jnp.maximum(values, -reach), reach).astype(kind)


def setup_inputs(seed: int = 0, part: int = 0) -> dict:
    key_of = jax.random.split(jax.random.key(seed), 12)
    part_splits = jax.random.split(jax.random.fold_in(key_of[11], part), 12)
    return {
        "patterns": gaussian(part_splits[0], (2, BOXES, K, R), 1.0, 6.0, ((1, 16),)),
        "owner_block": place_ends(jax.random.randint(key_of[1], (STEPS,), 0, BLOCKS), jax.random.fold_in(key_of[1], 1), 0, BLOCKS - 1).astype(jnp.int32),
        "low_index": place_ends(jax.random.randint(key_of[2], (BOXES, SRC), 0, NTRANS), jax.random.fold_in(key_of[2], 1), 0, NTRANS - 1).astype(jnp.int32),
        "low_mask": place_ends((jax.random.randint(key_of[3], (BOXES, SRC), 0, 2) < 1).astype(jnp.int32), jax.random.fold_in(key_of[3], 1), 0, 1),
        "low_table": gaussian(key_of[4], (2, NTRANS, K), 0.15, 2.0),
        "interp": gaussian(key_of[5], (K, Q), K ** -0.5, 0.5),
        "shift_angle": jnp.clip(jax.random.uniform(key_of[6], (8, Q), jnp.float32, -3.140625, 3.140625), -3.140625, 3.140625),
        "par_source": draw_par_source(jax.random.fold_in(key_of[11], 71), part),
        "par_index": place_ends(jax.random.randint(key_of[8], (PARENTS, PLIST), 0, NTRANS), jax.random.fold_in(key_of[8], 1), 0, NTRANS - 1).astype(jnp.int32),
        "par_mask": place_ends((jax.random.randint(key_of[9], (PARENTS, PLIST), 0, 4) < 3).astype(jnp.int32), jax.random.fold_in(key_of[9], 1), 0, 1),
        "par_table": gaussian(key_of[10], (2, NTRANS, Q), 0.1, 1.5),
    }


def complex_apply(operator, sources):
    left_real = operator[0].astype(jnp.float32)
    left_imaginary = operator[1].astype(jnp.float32)
    right_real = sources[0].astype(jnp.float32)
    right_imaginary = sources[1].astype(jnp.float32)
    real_part = jnp.einsum('bjk,jkr->bkr', left_real, right_real) - jnp.einsum('bjk,jkr->bkr', left_imaginary, right_imaginary)
    imaginary = jnp.einsum('bjk,jkr->bkr', left_real, right_imaginary) + jnp.einsum('bjk,jkr->bkr', left_imaginary, right_real)
    return jnp.stack([real_part, imaginary])


def reference(patterns, owner_block, low_index, low_mask, low_table, interp, shift_angle, par_source, par_index, par_mask, par_table):
    boxes = patterns.shape[1]
    clusters = boxes // BOX_DEV
    blocks_each = BOX_DEV // 8
    far_ids = (owner_block[:, None] * 8 + jnp.arange(8, dtype=jnp.int32)[None, :]).reshape(-1).astype(jnp.int32)
    far_patterns = patterns[:, far_ids]
    cosine = jnp.cos(shift_angle)
    sine = jnp.sin(shift_angle)
    interp_wide = interp.astype(jnp.float32)

    def lift_cluster(cluster):
        child = lax.dynamic_slice_in_dim(patterns, cluster * BOX_DEV, BOX_DEV, 1).astype(jnp.float32)
        lifted = jnp.einsum('cbkr,kq->cbqr', child, interp_wide)
        lifted = lifted.reshape(2, blocks_each, 8, Q, R)
        real_part = jnp.sum(cosine[None, :, :, None] * lifted[0] - sine[None, :, :, None] * lifted[1], axis=1)
        imaginary = jnp.sum(cosine[None, :, :, None] * lifted[1] + sine[None, :, :, None] * lifted[0], axis=1)
        return jnp.stack([real_part, imaginary]).astype(jnp.bfloat16)

    lifted_all = lax.map(lift_cluster, jnp.arange(clusters, dtype=jnp.int32))
    parent_patterns = jnp.transpose(lifted_all, (1, 0, 2, 3, 4)).reshape(2, PARENTS, Q, R)

    def add_slot(slot, total):
        source = par_source[:, slot]
        which = par_index[:, slot]
        weight = par_mask[:, slot].astype(jnp.float32)
        picked = parent_patterns[:, source].astype(jnp.float32)
        operator = par_table[:, which].astype(jnp.float32) * weight[None, :, None]
        real_part = operator[0][:, :, None] * picked[0] - operator[1][:, :, None] * picked[1]
        imaginary = operator[0][:, :, None] * picked[1] + operator[1][:, :, None] * picked[0]
        return total + jnp.stack([real_part, imaginary])

    translated = lax.fori_loop(0, PLIST, add_slot, jnp.zeros((2, PARENTS, Q, R), jnp.float32)).astype(jnp.bfloat16)

    def finish_cluster(cluster):
        own = lax.dynamic_slice_in_dim(patterns, cluster * BOX_DEV, BOX_DEV, 1)
        sources = jnp.concatenate([own, far_patterns], axis=1)
        index = lax.dynamic_slice_in_dim(low_index, cluster * BOX_DEV, BOX_DEV, 0)
        keep = lax.dynamic_slice_in_dim(low_mask, cluster * BOX_DEV, BOX_DEV, 0).astype(jnp.float32)
        operator = low_table[:, index].astype(jnp.float32) * keep[None, :, :, None]
        near = complex_apply(jnp.transpose(operator, (0, 1, 2, 3)), sources)
        parents_here = lax.dynamic_slice_in_dim(translated, cluster * blocks_each, blocks_each, 1).astype(jnp.float32)
        wide = parents_here[:, :, None]
        real_part = cosine[None, :, :, None] * wide[0] + sine[None, :, :, None] * wide[1]
        imaginary = cosine[None, :, :, None] * wide[1] - sine[None, :, :, None] * wide[0]
        phased = jnp.stack([real_part, imaginary]).astype(jnp.bfloat16).reshape(2, BOX_DEV, Q, R)
        down = jnp.einsum('cbqr,kq->cbkr', phased.astype(jnp.float32), interp_wide)
        return near + down

    result = lax.map(finish_cluster, jnp.arange(clusters, dtype=jnp.int32))
    return jnp.transpose(result, (1, 0, 2, 3, 4)).reshape(2, boxes, K, R)
```

```python
import functools

import jax
import jax.numpy as jnp
from jax import lax
from jax.experimental import pallas as pl
from jax.experimental.pallas import tpu as pltpu
from jax.sharding import PartitionSpec as P

F32 = jnp.float32
BF16 = jnp.bfloat16
MESH = pl.DeviceIdType.MESH


def dot(left, right):
    return jnp.dot(left, right, preferred_element_type=F32)


def kernel(
    n,
    listed,
    owner_ref,
    pat_ref,
    own_op_ref,
    far_op_ref,
    interp_ref,
    lift_ref,
    phase_ref,
    couple_ref,
    out_ref,
    parent,
    arrived,
    wide,
    result,
    result_send,
    returned,
    buf,
    landed,
    far,
    far_wide,
    own_wide,
    acc,
    out_send,
    out_recv,
    back_send,
    back_recv,
    rs_send,
    rs_recv,
    ag_send,
    ag_recv,
):
    me = lax.axis_index("box")
    boxes = pat_ref.shape[1]
    kdir, illums = pat_ref.shape[2], pat_ref.shape[3]
    groups8 = boxes // 8
    qdir = lift_ref.shape[0]
    qloc = qdir // n
    rows = 2 * listed * 8
    stages = n.bit_length() - 1

    barrier = pltpu.get_barrier_semaphore()

    def greet(i, carry):
        peer = lax.rem(me + i, n)
        pl.semaphore_signal(barrier, inc=1, device_id={"box": peer}, device_id_type=MESH)
        return carry

    lax.fori_loop(1, n, greet, 0)

    for step in range(listed):
        owner = owner_ref[step]
        mine = owner // groups8 == me
        first = owner % groups8 * 8
        for part in range(2):
            block = pat_ref[part, pl.ds(first, 8)]
            buf[pl.ds((part * listed + step) * 8, 8)] = jnp.where(mine, block, jnp.zeros_like(block))

    pl.semaphore_wait(barrier, n - 1)

    def halving(stage):
        size = rows >> (stage + 1)
        low = 0
        for s in range(stage):
            low = low + (me // (1 << s) % 2) * (rows >> (s + 1))
        bit = me // (1 << stage) % 2
        keep = low + bit * size
        give = low + (1 - bit) * size
        partner = me + (1 - 2 * bit) * (1 << stage)
        spot = rows - 2 * size
        copy = pltpu.make_async_remote_copy(
            src_ref=buf.at[pl.ds(give, size)],
            dst_ref=landed.at[pl.ds(spot, size)],
            send_sem=rs_send.at[stage],
            recv_sem=rs_recv.at[stage],
            device_id={"box": partner},
            device_id_type=MESH,
        )

        def finish(last):
            copy.wait()
            target = far if last else buf
            target[pl.ds(keep, size)] = buf[pl.ds(keep, size)] + landed[pl.ds(spot, size)]

        return copy, finish

    def doubling(stage):
        size = rows >> (stage + 1)
        low = 0
        for s in range(stage + 1):
            low = low + (me // (1 << s) % 2) * (rows >> (s + 1))
        bit = me // (1 << stage) % 2
        partner = me + (1 - 2 * bit) * (1 << stage)
        return pltpu.make_async_remote_copy(
            src_ref=far.at[pl.ds(low, size)],
            dst_ref=far.at[pl.ds(low, size)],
            send_sem=ag_send.at[stage],
            recv_sem=ag_recv.at[stage],
            device_id={"box": partner},
            device_id_type=MESH,
        )

    copies = [None] * stages
    copies[0] = halving(0)
    copies[0][0].start()

    tile = 256
    for parent_at in range(groups8):

        def lift(t, carry, parent_at=parent_at):
            at = pl.multiple_of(t * tile, tile)
            left = lift_ref[pl.ds(at, tile), :]
            real = jnp.zeros((tile, illums), F32)
            imag = jnp.zeros((tile, illums), F32)
            for child in range(8):
                b = parent_at * 8 + child
                both = dot(left, jnp.concatenate([pat_ref[0, b], pat_ref[1, b]], axis=1))
                cosine = phase_ref[pl.ds(at, tile), child : child + 1]
                sine = phase_ref[pl.ds(at, tile), 8 + child : 9 + child]
                re, im = both[:, :illums], both[:, illums:]
                real = real + (cosine * re - sine * im)
                imag = imag + (cosine * im + sine * re)
            parent[parent_at, pl.ds(at, tile), :] = real.astype(BF16)
            parent[groups8 + parent_at, pl.ds(at, tile), :] = imag.astype(BF16)
            return carry

        lax.fori_loop(0, qdir // tile, lift, 0)

    def out_copy(i):
        peer = lax.rem(me + i, n)
        return pltpu.make_async_remote_copy(
            src_ref=parent.at[:, pl.ds(pl.multiple_of(peer * qloc, qloc), qloc), :],
            dst_ref=arrived.at[me],
            send_sem=out_send.at[i],
            recv_sem=out_recv.at[i],
            device_id={"box": peer},
            device_id_type=MESH,
        )

    def start_out(i, carry):
        out_copy(i).start()
        return carry

    lax.fori_loop(1, n, start_out, 0)

    copies[0][1](stages == 1)
    if stages > 1:
        copies[1] = halving(1)
        copies[1][0].start()

    for part in range(2):
        for b in range(boxes):
            own_wide[pl.ds((part * boxes + b) * kdir, kdir), :] = pat_ref[part, b].astype(F32)
    unroll = 4

    def near_own(t, carry):
        for u in range(unroll):
            k = t * unroll + u
            sources = own_wide[pl.ds(k, 2 * boxes, stride=kdir), :].astype(BF16)
            acc[pl.ds(k, 2 * boxes, stride=kdir), :] = dot(own_op_ref[k], sources)
        return carry

    lax.fori_loop(0, kdir // unroll, near_own, 0)

    def widen(source, value):
        for part in range(2):
            for p in range(groups8):
                s = (part * n + source) * groups8 + p
                at = pl.multiple_of(s * qloc, qloc)
                wide[pl.ds(at, qloc), :] = value(part * groups8 + p).astype(F32)

    widen(me, lambda c: parent[c, pl.ds(pl.multiple_of(me * qloc, qloc), qloc), :])

    def take(i, carry):
        out_copy(i).wait()
        source = lax.rem(me - i + n, n)
        widen(source, lambda c: arrived[source, c])
        return carry

    lax.fori_loop(1, n, take, 0)
    parents2 = 2 * n * groups8

    def translate(t, carry):
        for u in range(unroll):
            q = t * unroll + u
            sources = wide[pl.ds(q, parents2, stride=qloc), :].astype(BF16)
            result[pl.ds(q, parents2, stride=qloc), :] = dot(couple_ref[q], sources)
        return carry

    lax.fori_loop(0, qloc // unroll, translate, 0)
    result_send[...] = result[...].reshape(2, n * groups8, qloc, illums).astype(BF16)

    def back_copy(i):
        peer = lax.rem(me + i, n)
        return pltpu.make_async_remote_copy(
            src_ref=result_send.at[:, pl.ds(peer * groups8, groups8)],
            dst_ref=returned.at[:, :, pl.ds(pl.multiple_of(me * qloc, qloc), qloc), :],
            send_sem=back_send.at[i],
            recv_sem=back_recv.at[i],
            device_id={"box": peer},
            device_id_type=MESH,
        )

    def start_back(i, carry):
        back_copy(i).start()
        return carry

    lax.fori_loop(1, n, start_back, 0)
    returned[:, :, pl.ds(pl.multiple_of(me * qloc, qloc), qloc), :] = result_send[:, pl.ds(me * groups8, groups8)]

    for stage in range(1, stages):
        copies[stage][1](stage == stages - 1)
        if stage + 1 < stages:
            copies[stage + 1] = halving(stage + 1)
            copies[stage + 1][0].start()
    for stage in reversed(range(stages)):
        copy = doubling(stage)
        copy.start()
        copy.wait()

    def widen_far(j, carry):
        far_wide[pl.ds(pl.multiple_of(j * kdir, kdir), kdir), :] = far[j].astype(F32)
        return carry

    lax.fori_loop(0, rows, widen_far, 0)

    def near_far(t, carry):
        for u in range(unroll):
            k = t * unroll + u
            sources = far_wide[pl.ds(k, rows, stride=kdir), :].astype(BF16)
            spots = pl.ds(k, 2 * boxes, stride=kdir)
            acc[spots, :] = acc[spots, :] + dot(far_op_ref[k], sources)
        return carry

    lax.fori_loop(0, kdir // unroll, near_far, 0)

    def land(i, carry):
        back_copy(i).wait()
        return carry

    lax.fori_loop(1, n, land, 0)

    for parent_at in range(groups8):
        for child in range(8):
            b = parent_at * 8 + child
            re = returned[0, parent_at].astype(F32)
            im = returned[1, parent_at].astype(F32)
            cosine = phase_ref[:, child : child + 1]
            sine = phase_ref[:, 8 + child : 9 + child]
            real = (cosine * re + sine * im).astype(BF16)
            imag = (cosine * im - sine * re).astype(BF16)
            both = dot(interp_ref[...], jnp.concatenate([real, imag], axis=1))
            out_ref[0, b] = acc[pl.ds(b * kdir, kdir), :] + both[:, :illums]
            out_ref[1, b] = acc[pl.ds((boxes + b) * kdir, kdir), :] + both[:, illums:]


def block_complex(real, imag):
    top = jnp.concatenate([real, -imag], axis=2)
    bottom = jnp.concatenate([imag, real], axis=2)
    return jnp.concatenate([top, bottom], axis=1)


def shards(
    patterns,
    owner_block,
    low_index,
    low_mask,
    low_table,
    interp,
    shift_angle,
    par_source,
    par_index,
    par_mask,
    par_table,
):
    boxes, kdir, illums = patterns.shape[1:]
    groups8 = boxes // 8
    qdir = interp.shape[1]
    n = lax.axis_size("box")
    listed = owner_block.shape[0]
    parents = par_source.shape[0]
    qloc = qdir // n
    rows = 2 * listed * 8
    sources = low_index.shape[1]

    ntrans = low_table.shape[1]
    kinds = jnp.arange(ntrans, dtype=jnp.int32)
    low_code = jnp.where(low_mask > 0, low_index, -1)
    low_hot = (low_code[:, :, None] == kinds).astype(BF16).reshape(boxes * sources, ntrans)
    low_op = jnp.einsum("ctk,nt->ckn", low_table, low_hot, preferred_element_type=F32)
    low_op = low_op.astype(BF16).reshape(2, kdir, boxes, sources)
    own_op = block_complex(low_op[0, :, :, :boxes], low_op[1, :, :, :boxes])
    far_op = block_complex(low_op[0, :, :, boxes:], low_op[1, :, :, boxes:])

    start = lax.axis_index("box") * qloc
    table = lax.dynamic_slice_in_dim(par_table, start, qloc, 2)
    match = par_source[:, :, None] == jnp.arange(parents, dtype=jnp.int32)
    match = match & (par_mask[:, :, None] > 0)
    par_code = jnp.sum(jnp.where(match, par_index[:, :, None] + 1, 0), axis=1) - 1
    par_kinds = jnp.arange(par_table.shape[1], dtype=jnp.int32)
    par_hot = (par_code[:, :, None] == par_kinds).astype(BF16).reshape(parents * parents, -1)
    couple = jnp.einsum("ctq,nt->cqn", table, par_hot, preferred_element_type=F32)
    couple = couple.astype(BF16).reshape(2, qloc, parents, parents)
    couple = block_complex(couple[0], couple[1])

    phase = jnp.concatenate([jnp.cos(shift_angle), jnp.sin(shift_angle)], axis=0).T

    vmem = pl.BlockSpec(memory_space=pltpu.VMEM)
    smem = pl.BlockSpec(memory_space=pltpu.SMEM)
    stages = n.bit_length() - 1
    dma = pltpu.SemaphoreType.DMA
    return pl.pallas_call(
        functools.partial(kernel, n, listed),
        out_shape=jax.ShapeDtypeStruct((2, boxes, kdir, illums), F32),
        in_specs=[smem] + [vmem] * 7,
        out_specs=vmem,
        scratch_shapes=[
            pltpu.VMEM((2 * groups8, qdir, illums), BF16),
            pltpu.VMEM((n, 2 * groups8, qloc, illums), BF16),
            pltpu.VMEM((2 * parents * qloc, illums), F32),
            pltpu.VMEM((2 * parents * qloc, illums), F32),
            pltpu.VMEM((2, parents, qloc, illums), BF16),
            pltpu.VMEM((2, groups8, qdir, illums), BF16),
            pltpu.VMEM((rows, kdir, illums), BF16),
            pltpu.VMEM((rows, kdir, illums), BF16),
            pltpu.VMEM((rows, kdir, illums), BF16),
            pltpu.VMEM((rows * kdir, illums), F32),
            pltpu.VMEM((2 * boxes * kdir, illums), F32),
            pltpu.VMEM((2 * boxes * kdir, illums), F32),
            dma((n,)),
            dma((n,)),
            dma((n,)),
            dma((n,)),
            dma((stages,)),
            dma((stages,)),
            dma((stages,)),
            dma((stages,)),
        ],
        compiler_params=pltpu.CompilerParams(
            collective_id=0, has_side_effects=True, vmem_limit_bytes=56 * 1024 * 1024
        ),
    )(owner_block, patterns, own_op, far_op, interp, interp.T, phase, couple)


def solution(mesh):
    placed = (
        P(None, "box", None, "illum"),
        P(),
        P("box", None),
        P("box", None),
        P(),
        P(),
        P(),
        P(),
        P(),
        P(),
        P(),
    )
    return jax.shard_map(
        shards, mesh=mesh, in_specs=placed, out_specs=P(None, "box", None, "illum"), check_vma=False
    )
```

```python
import functools

import jax
import jax.numpy as jnp
from jax import lax
from jax.experimental import pallas as pl
from jax.experimental.pallas import tpu as pltpu
from jax.sharding import PartitionSpec as P

F32 = jnp.float32
BF16 = jnp.bfloat16
MESH = pl.DeviceIdType.MESH


def dot(left, right):
    return jnp.dot(left, right, preferred_element_type=F32)


def kernel(
    n,
    listed,
    owner_ref,
    pat_ref,
    own_op_ref,
    far_op_ref,
    interp_ref,
    lift_ref,
    phase_ref,
    couple_ref,
    out_ref,
    parent,
    arrived,
    wide,
    result,
    result_send,
    returned,
    buf,
    landed,
    far,
    far_wide,
    own_wide,
    out_send,
    out_recv,
    back_send,
    back_recv,
    rs_send,
    rs_recv,
    ag_send,
    ag_recv,
):
    me = lax.axis_index("box")
    boxes = pat_ref.shape[1]
    kdir, illums = pat_ref.shape[2], pat_ref.shape[3]
    groups8 = boxes // 8
    qdir = lift_ref.shape[0]
    qloc = qdir // n
    rows = 2 * listed * 8
    stages = n.bit_length() - 1

    barrier = pltpu.get_barrier_semaphore()

    def greet(i, carry):
        peer = lax.rem(me + i, n)
        pl.semaphore_signal(barrier, inc=1, device_id={"box": peer}, device_id_type=MESH)
        return carry

    lax.fori_loop(1, n, greet, 0)

    for step in range(listed):
        owner = owner_ref[step]
        mine = owner // groups8 == me
        first = owner % groups8 * 8
        for part in range(2):
            block = pat_ref[part, pl.ds(first, 8)]
            buf[pl.ds((part * listed + step) * 8, 8)] = jnp.where(mine, block, jnp.zeros_like(block))

    pl.semaphore_wait(barrier, n - 1)

    half = rows // 2
    later = list(range(1, stages))
    cut = (stages + 1) // 2
    chains = [later, [b for b in later if b >= cut] + [b for b in later if b < cut]]

    def place(chain, depth):
        low = me % 2 * half + chain * (half // 2)
        size = half // 2
        for b in chains[chain][:depth]:
            size = size // 2
            low = low + me // (1 << b) % 2 * size
        return low, size

    def remote(src, dst, send, recv, bit):
        mine = me // (1 << bit) % 2
        return pltpu.make_async_remote_copy(
            src_ref=src,
            dst_ref=dst,
            send_sem=send,
            recv_sem=recv,
            device_id={"box": me + (1 - 2 * mine) * (1 << bit)},
            device_id_type=MESH,
        )

    def first_swap():
        give = (1 - me % 2) * half
        return remote(
            buf.at[pl.ds(give, half)], landed.at[pl.ds(0, half)], rs_send.at[0, 0], rs_recv.at[0, 0], 0
        )

    def halving(chain, depth):
        bit = chains[chain][depth]
        low, size = place(chain, depth)
        size = size // 2
        give = low + (1 - me // (1 << bit) % 2) * size
        spot = half + chain * (half // 2) + half // 2 - 2 * size
        return remote(
            buf.at[pl.ds(give, size)],
            landed.at[pl.ds(spot, size)],
            rs_send.at[chain, 1 + depth],
            rs_recv.at[chain, 1 + depth],
            bit,
        )

    def halve(chain, depth):
        halving(chain, depth).wait()
        low, size = place(chain, depth + 1)
        spot = half + chain * (half // 2) + half // 2 - 2 * size
        target = far if depth + 1 == len(later) else buf
        target[pl.ds(low, size)] = buf[pl.ds(low, size)] + landed[pl.ds(spot, size)]
        if depth + 1 < len(later):
            halving(chain, depth + 1).start()
        else:
            doubling(chain, len(later)).start()

    def doubling(chain, depth):
        low, size = place(chain, depth)
        bit = chains[chain][depth - 1] if depth else 0
        spots = far.at[pl.ds(low, size)]
        return remote(spots, spots, ag_send.at[chain, depth], ag_recv.at[chain, depth], bit)

    def double(chain, depth):
        doubling(chain, depth).wait()
        doubling(chain, depth - 1).start()

    first_swap().start()

    tile = 256
    for parent_at in range(groups8):

        def lift(t, carry, parent_at=parent_at):
            at = pl.multiple_of(t * tile, tile)
            left = lift_ref[pl.ds(at, tile), :]
            real = jnp.zeros((tile, illums), F32)
            imag = jnp.zeros((tile, illums), F32)
            for child in range(8):
                b = parent_at * 8 + child
                both = dot(left, jnp.concatenate([pat_ref[0, b], pat_ref[1, b]], axis=1))
                cosine = phase_ref[pl.ds(at, tile), child : child + 1]
                sine = phase_ref[pl.ds(at, tile), 8 + child : 9 + child]
                re, im = both[:, :illums], both[:, illums:]
                real = real + (cosine * re - sine * im)
                imag = imag + (cosine * im + sine * re)
            parent[parent_at, pl.ds(at, tile), :] = real.astype(BF16)
            parent[groups8 + parent_at, pl.ds(at, tile), :] = imag.astype(BF16)
            return carry

        lax.fori_loop(0, qdir // tile, lift, 0)

    def out_copy(i):
        peer = lax.rem(me + i, n)
        return pltpu.make_async_remote_copy(
            src_ref=parent.at[:, pl.ds(pl.multiple_of(peer * qloc, qloc), qloc), :],
            dst_ref=arrived.at[me],
            send_sem=out_send.at[i],
            recv_sem=out_recv.at[i],
            device_id={"box": peer},
            device_id_type=MESH,
        )

    def start_out(i, carry):
        out_copy(i).start()
        return carry

    lax.fori_loop(1, n, start_out, 0)

    first_swap().wait()
    kept = pl.ds(me % 2 * half, half)
    buf[kept] = buf[kept] + landed[pl.ds(0, half)]
    halving(0, 0).start()
    halving(1, 0).start()

    for part in range(2):
        for b in range(boxes):
            own_wide[pl.ds((part * boxes + b) * kdir, kdir), :] = pat_ref[part, b].astype(F32)
    unroll = 4

    def near_own(t, carry):
        for u in range(unroll):
            k = t * unroll + u
            sources = own_wide[pl.ds(k, 2 * boxes, stride=kdir), :].astype(BF16)
            out_ref[pl.ds(k, 2 * boxes, stride=kdir), :] = dot(own_op_ref[k], sources)
        return carry

    lax.fori_loop(0, kdir // unroll, near_own, 0)

    for chain in range(2):
        halve(chain, 0)

    def widen(source, value):
        for part in range(2):
            for p in range(groups8):
                s = (part * n + source) * groups8 + p
                at = pl.multiple_of(s * qloc, qloc)
                wide[pl.ds(at, qloc), :] = value(part * groups8 + p).astype(F32)

    widen(me, lambda c: parent[c, pl.ds(pl.multiple_of(me * qloc, qloc), qloc), :])

    def take(i, carry):
        out_copy(i).wait()
        source = lax.rem(me - i + n, n)
        widen(source, lambda c: arrived[source, c])
        return carry

    lax.fori_loop(1, n, take, 0)
    parents2 = 2 * n * groups8

    def translate(t, carry):
        for u in range(unroll):
            q = t * unroll + u
            sources = wide[pl.ds(q, parents2, stride=qloc), :].astype(BF16)
            result[pl.ds(q, parents2, stride=qloc), :] = dot(couple_ref[q], sources)
        return carry

    lax.fori_loop(0, qloc // unroll, translate, 0)
    result_send[...] = result[...].reshape(2, n * groups8, qloc, illums).astype(BF16)

    def back_copy(i):
        peer = lax.rem(me + i, n)
        return pltpu.make_async_remote_copy(
            src_ref=result_send.at[:, pl.ds(peer * groups8, groups8)],
            dst_ref=returned.at[:, :, pl.ds(pl.multiple_of(me * qloc, qloc), qloc), :],
            send_sem=back_send.at[i],
            recv_sem=back_recv.at[i],
            device_id={"box": peer},
            device_id_type=MESH,
        )

    def start_back(i, carry):
        back_copy(i).start()
        return carry

    lax.fori_loop(1, n, start_back, 0)
    returned[:, :, pl.ds(pl.multiple_of(me * qloc, qloc), qloc), :] = result_send[:, pl.ds(me * groups8, groups8)]

    for depth in range(1, len(later)):
        for chain in range(2):
            halve(chain, depth)
    for depth in range(len(later), 1, -1):
        for chain in range(2):
            double(chain, depth)

    def land(i, carry):
        back_copy(i).wait()
        return carry

    lax.fori_loop(1, n, land, 0)

    for parent_at in range(groups8):
        for child in range(8):
            b = parent_at * 8 + child
            re = returned[0, parent_at].astype(F32)
            im = returned[1, parent_at].astype(F32)
            cosine = phase_ref[:, child : child + 1]
            sine = phase_ref[:, 8 + child : 9 + child]
            real = (cosine * re + sine * im).astype(BF16)
            imag = (cosine * im - sine * re).astype(BF16)
            both = dot(interp_ref[...], jnp.concatenate([real, imag], axis=1))
            spots = pl.ds(b * kdir, kdir)
            out_ref[spots, :] = out_ref[spots, :] + both[:, :illums]
            spots = pl.ds((boxes + b) * kdir, kdir)
            out_ref[spots, :] = out_ref[spots, :] + both[:, illums:]

    for chain in range(2):
        double(chain, 1)

    def near_half(part):
        def widen_far(j, carry):
            far_wide[pl.ds(pl.multiple_of(j * kdir, kdir), kdir), :] = far[part * half + j].astype(F32)
            return carry

        lax.fori_loop(0, half, widen_far, 0)

        def near_far(t, carry):
            for u in range(unroll):
                k = t * unroll + u
                sources = far_wide[pl.ds(k, half, stride=kdir), :].astype(BF16)
                spots = pl.ds(k, 2 * boxes, stride=kdir)
                out_ref[spots, :] = out_ref[spots, :] + dot(far_op_ref[part, k], sources)
            return carry

        lax.fori_loop(0, kdir // unroll, near_far, 0)

    near_half(me % 2)
    for chain in range(2):
        doubling(chain, 0).wait()
    near_half(1 - me % 2)


def block_complex(real, imag):
    top = jnp.concatenate([real, -imag], axis=2)
    bottom = jnp.concatenate([imag, real], axis=2)
    return jnp.concatenate([top, bottom], axis=1)


def shards(
    patterns,
    owner_block,
    low_index,
    low_mask,
    low_table,
    interp,
    shift_angle,
    par_source,
    par_index,
    par_mask,
    par_table,
):
    boxes, kdir, illums = patterns.shape[1:]
    groups8 = boxes // 8
    qdir = interp.shape[1]
    n = lax.axis_size("box")
    listed = owner_block.shape[0]
    parents = par_source.shape[0]
    qloc = qdir // n
    rows = 2 * listed * 8
    sources = low_index.shape[1]

    ntrans = low_table.shape[1]
    kinds = jnp.arange(ntrans, dtype=jnp.int32)
    low_code = jnp.where(low_mask > 0, low_index, -1)
    low_hot = (low_code[:, :, None] == kinds).astype(BF16).reshape(boxes * sources, ntrans)
    low_op = jnp.einsum("ctk,nt->ckn", low_table, low_hot, preferred_element_type=F32)
    low_op = low_op.astype(BF16).reshape(2, kdir, boxes, sources)
    own_op = block_complex(low_op[0, :, :, :boxes], low_op[1, :, :, :boxes])
    far_real, far_imag = low_op[0, :, :, boxes:], low_op[1, :, :, boxes:]
    far_op = jnp.stack(
        [
            jnp.concatenate([far_real, far_imag], axis=1),
            jnp.concatenate([-far_imag, far_real], axis=1),
        ]
    )

    start = lax.axis_index("box") * qloc
    table = lax.dynamic_slice_in_dim(par_table, start, qloc, 2)
    match = par_source[:, :, None] == jnp.arange(parents, dtype=jnp.int32)
    match = match & (par_mask[:, :, None] > 0)
    par_code = jnp.sum(jnp.where(match, par_index[:, :, None] + 1, 0), axis=1) - 1
    par_kinds = jnp.arange(par_table.shape[1], dtype=jnp.int32)
    par_hot = (par_code[:, :, None] == par_kinds).astype(BF16).reshape(parents * parents, -1)
    couple = jnp.einsum("ctq,nt->cqn", table, par_hot, preferred_element_type=F32)
    couple = couple.astype(BF16).reshape(2, qloc, parents, parents)
    couple = block_complex(couple[0], couple[1])

    phase = jnp.concatenate([jnp.cos(shift_angle), jnp.sin(shift_angle)], axis=0).T

    vmem = pl.BlockSpec(memory_space=pltpu.VMEM)
    smem = pl.BlockSpec(memory_space=pltpu.SMEM)
    stages = n.bit_length() - 1
    dma = pltpu.SemaphoreType.DMA
    return pl.pallas_call(
        functools.partial(kernel, n, listed),
        out_shape=jax.ShapeDtypeStruct((2 * boxes * kdir, illums), F32),
        in_specs=[smem] + [vmem] * 7,
        out_specs=vmem,
        scratch_shapes=[
            pltpu.VMEM((2 * groups8, qdir, illums), BF16),
            pltpu.VMEM((n, 2 * groups8, qloc, illums), BF16),
            pltpu.VMEM((2 * parents * qloc, illums), F32),
            pltpu.VMEM((2 * parents * qloc, illums), F32),
            pltpu.VMEM((2, parents, qloc, illums), BF16),
            pltpu.VMEM((2, groups8, qdir, illums), BF16),
            pltpu.VMEM((rows, kdir, illums), BF16),
            pltpu.VMEM((rows, kdir, illums), BF16),
            pltpu.VMEM((rows, kdir, illums), BF16),
            pltpu.VMEM((rows // 2 * kdir, illums), F32),
            pltpu.VMEM((2 * boxes * kdir, illums), F32),
            dma((n,)),
            dma((n,)),
            dma((n,)),
            dma((n,)),
            dma((2, stages)),
            dma((2, stages)),
            dma((2, stages)),
            dma((2, stages)),
        ],
        compiler_params=pltpu.CompilerParams(
            collective_id=0, has_side_effects=True, vmem_limit_bytes=56 * 1024 * 1024
        ),
    )(owner_block, patterns, own_op, far_op, interp, interp.T, phase, couple).reshape(2, boxes, kdir, illums)


def solution(mesh):
    placed = (
        P(None, "box", None, "illum"),
        P(),
        P("box", None),
        P("box", None),
        P(),
        P(),
        P(),
        P(),
        P(),
        P(),
        P(),
    )
    return jax.shard_map(
        shards, mesh=mesh, in_specs=placed, out_specs=P(None, "box", None, "illum"), check_vma=False
    )
```

```python
import functools

import jax
import jax.numpy as jnp
from jax import lax
from jax.experimental import pallas as pl
from jax.experimental.pallas import tpu as pltpu
from jax.sharding import PartitionSpec as P

F32 = jnp.float32
BF16 = jnp.bfloat16
MESH = pl.DeviceIdType.MESH


def dot(left, right):
    return jnp.dot(left, right, preferred_element_type=F32)


def kernel(
    n,
    listed,
    owner_ref,
    pat_ref,
    code_ref,
    table_ref,
    source_ref,
    index_ref,
    mask_ref,
    par_ref,
    interp_ref,
    phase_ref,
    out_ref,
    op,
    couple,
    parent,
    arrived,
    wide,
    result,
    result_send,
    returned,
    buf,
    landed,
    far,
    far_wide,
    own_wide,
    out_send,
    out_recv,
    back_send,
    back_recv,
    rs_send,
    rs_recv,
    ag_send,
    ag_recv,
):
    me = lax.axis_index("box")
    boxes = pat_ref.shape[1]
    kdir, illums = pat_ref.shape[2], pat_ref.shape[3]
    groups8 = boxes // 8
    qdir = interp_ref.shape[1]
    qloc = qdir // n
    rows = 2 * listed * 8
    stages = n.bit_length() - 1

    barrier = pltpu.get_barrier_semaphore()

    def greet(i, carry):
        peer = lax.rem(me + i, n)
        pl.semaphore_signal(barrier, inc=1, device_id={"box": peer}, device_id_type=MESH)
        return carry

    lax.fori_loop(1, n, greet, 0)

    for step in range(listed):
        owner = owner_ref[step]
        mine = owner // groups8 == me
        first = owner % groups8 * 8
        for part in range(2):
            block = pat_ref[part, pl.ds(first, 8)]
            buf[pl.ds((part * listed + step) * 8, 8)] = jnp.where(mine, block, jnp.zeros_like(block))

    pl.semaphore_wait(barrier, n - 1)

    half = rows // 2
    later = list(range(1, stages))
    cut = (stages + 1) // 2
    chains = [later, [b for b in later if b >= cut] + [b for b in later if b < cut]]

    def place(chain, depth):
        low = me % 2 * half + chain * (half // 2)
        size = half // 2
        for b in chains[chain][:depth]:
            size = size // 2
            low = low + me // (1 << b) % 2 * size
        return low, size

    def remote(src, dst, send, recv, bit):
        mine = me // (1 << bit) % 2
        return pltpu.make_async_remote_copy(
            src_ref=src,
            dst_ref=dst,
            send_sem=send,
            recv_sem=recv,
            device_id={"box": me + (1 - 2 * mine) * (1 << bit)},
            device_id_type=MESH,
        )

    def first_swap():
        give = (1 - me % 2) * half
        return remote(
            buf.at[pl.ds(give, half)], landed.at[pl.ds(0, half)], rs_send.at[0, 0], rs_recv.at[0, 0], 0
        )

    def halving(chain, depth):
        bit = chains[chain][depth]
        low, size = place(chain, depth)
        size = size // 2
        give = low + (1 - me // (1 << bit) % 2) * size
        spot = half + chain * (half // 2) + half // 2 - 2 * size
        return remote(
            buf.at[pl.ds(give, size)],
            landed.at[pl.ds(spot, size)],
            rs_send.at[chain, 1 + depth],
            rs_recv.at[chain, 1 + depth],
            bit,
        )

    def halve(chain, depth):
        halving(chain, depth).wait()
        low, size = place(chain, depth + 1)
        spot = half + chain * (half // 2) + half // 2 - 2 * size
        target = far if depth + 1 == len(later) else buf
        target[pl.ds(low, size)] = buf[pl.ds(low, size)] + landed[pl.ds(spot, size)]
        if depth + 1 < len(later):
            halving(chain, depth + 1).start()
        else:
            doubling(chain, len(later)).start()

    def doubling(chain, depth):
        low, size = place(chain, depth)
        bit = chains[chain][depth - 1] if depth else 0
        spots = far.at[pl.ds(low, size)]
        return remote(spots, spots, ag_send.at[chain, depth], ag_recv.at[chain, depth], bit)

    def double(chain, depth):
        doubling(chain, depth).wait()
        doubling(chain, depth - 1).start()

    first_swap().start()

    tile = 256
    for parent_at in range(groups8):

        def lift(t, carry, parent_at=parent_at):
            at = pl.multiple_of(t * tile, tile)
            left = interp_ref[:, pl.ds(at, tile)].T
            real = jnp.zeros((tile, illums), F32)
            imag = jnp.zeros((tile, illums), F32)
            for child in range(8):
                b = parent_at * 8 + child
                both = dot(left, jnp.concatenate([pat_ref[0, b], pat_ref[1, b]], axis=1))
                cosine = phase_ref[pl.ds(at, tile), child : child + 1]
                sine = phase_ref[pl.ds(at, tile), 8 + child : 9 + child]
                re, im = both[:, :illums], both[:, illums:]
                real = real + (cosine * re - sine * im)
                imag = imag + (cosine * im + sine * re)
            parent[parent_at, pl.ds(at, tile), :] = real.astype(BF16)
            parent[groups8 + parent_at, pl.ds(at, tile), :] = imag.astype(BF16)
            return carry

        lax.fori_loop(0, qdir // tile, lift, 0)

    def out_copy(i):
        peer = lax.rem(me + i, n)
        return pltpu.make_async_remote_copy(
            src_ref=parent.at[:, pl.ds(pl.multiple_of(peer * qloc, qloc), qloc), :],
            dst_ref=arrived.at[me],
            send_sem=out_send.at[i],
            recv_sem=out_recv.at[i],
            device_id={"box": peer},
            device_id_type=MESH,
        )

    def start_out(i, carry):
        out_copy(i).start()
        return carry

    lax.fori_loop(1, n, start_out, 0)

    first_swap().wait()
    kept = pl.ds(me % 2 * half, half)
    buf[kept] = buf[kept] + landed[pl.ds(0, half)]
    halving(0, 0).start()
    halving(1, 0).start()

    unroll = 4
    parents = n * groups8
    parents2 = 2 * parents

    lanes = lax.broadcasted_iota(jnp.int32, (parents, parents), 1)
    code = jnp.zeros((parents, parents), jnp.int32)
    slot_code = jnp.where(mask_ref[...] > 0, index_ref[...] + 1, 0)
    for j in range(source_ref.shape[1]):
        code = code + jnp.where(source_ref[:, j : j + 1] == lanes, slot_code[:, j : j + 1], 0)
    code = jnp.concatenate([code, code], axis=1) - 1
    each = max(1, 256 // parents2)
    kinds = lax.broadcasted_iota(jnp.int32, (par_ref.shape[1], each * parents2), 0)
    first = lax.broadcasted_iota(jnp.int32, (qloc, parents2), 1) < parents
    for p in range(0, parents, each):
        row = jnp.concatenate([code[p + u : p + u + 1] for u in range(each)], axis=1)
        hot = jnp.where(kinds == row, 1.0, 0.0).astype(BF16)
        got = dot(par_ref[...], hot)
        for u in range(each):
            real = got[:qloc, u * parents2 : (u + 1) * parents2]
            imag = got[qloc:, u * parents2 : (u + 1) * parents2]
            couple[pl.ds(p + u, qloc, stride=parents2), :] = jnp.where(first, real, -imag)
            couple[pl.ds(parents + p + u, qloc, stride=parents2), :] = jnp.where(first, imag, real)

    width = code_ref.shape[1]
    low_kinds = lax.broadcasted_iota(jnp.int32, (table_ref.shape[1], 2 * width), 0)
    lane = lax.broadcasted_iota(jnp.int32, (kdir, width), 1)
    flip = me % 2
    column = jnp.where(
        lane < 2 * boxes, lane // boxes, jnp.where(lane < 2 * boxes + half, flip, 1 - flip)
    )
    low_first = column == 0
    for b in range(0, boxes, 2):
        row = jnp.concatenate([code_ref[b : b + 1], code_ref[b + 1 : b + 2]], axis=1)
        hot = jnp.where(low_kinds == row, 1.0, 0.0).astype(BF16)
        got = dot(table_ref[...], hot)
        for u in range(2):
            real = got[:kdir, u * width : (u + 1) * width]
            imag = got[kdir:, u * width : (u + 1) * width]
            op[pl.ds(b + u, kdir, stride=2 * boxes), :] = jnp.where(low_first, real, -imag)
            op[pl.ds(boxes + b + u, kdir, stride=2 * boxes), :] = jnp.where(low_first, imag, real)

    def operator(k):
        return op[pl.ds(pl.multiple_of(k * 2 * boxes, 2 * boxes), 2 * boxes), :].astype(BF16)

    for chain in range(2):
        halve(chain, 0)

    def widen(source, value):
        for part in range(2):
            for p in range(groups8):
                s = (part * n + source) * groups8 + p
                at = pl.multiple_of(s * qloc, qloc)
                wide[pl.ds(at, qloc), :] = value(part * groups8 + p).astype(F32)

    widen(me, lambda c: parent[c, pl.ds(pl.multiple_of(me * qloc, qloc), qloc), :])

    def take(i, carry):
        out_copy(i).wait()
        source = lax.rem(me - i + n, n)
        widen(source, lambda c: arrived[source, c])
        return carry

    lax.fori_loop(1, n, take, 0)
    def translate(t, carry):
        for u in range(unroll):
            q = t * unroll + u
            sources = wide[pl.ds(q, parents2, stride=qloc), :].astype(BF16)
            result[pl.ds(q, parents2, stride=qloc), :] = dot(
                couple[pl.ds(pl.multiple_of(q * parents2, parents2), parents2), :].astype(BF16), sources
            )
        return carry

    lax.fori_loop(0, qloc // unroll, translate, 0)
    result_send[...] = result[...].reshape(2, n * groups8, qloc, illums).astype(BF16)

    def back_copy(i):
        peer = lax.rem(me + i, n)
        return pltpu.make_async_remote_copy(
            src_ref=result_send.at[:, pl.ds(peer * groups8, groups8)],
            dst_ref=returned.at[:, :, pl.ds(pl.multiple_of(me * qloc, qloc), qloc), :],
            send_sem=back_send.at[i],
            recv_sem=back_recv.at[i],
            device_id={"box": peer},
            device_id_type=MESH,
        )

    def start_back(i, carry):
        back_copy(i).start()
        return carry

    lax.fori_loop(1, n, start_back, 0)
    returned[:, :, pl.ds(pl.multiple_of(me * qloc, qloc), qloc), :] = result_send[:, pl.ds(me * groups8, groups8)]

    for chain in range(2):
        halve(chain, 1)

    for part in range(2):
        for b in range(boxes):
            own_wide[pl.ds((part * boxes + b) * kdir, kdir), :] = pat_ref[part, b].astype(F32)

    def near_own(t, carry):
        for u in range(unroll):
            k = t * unroll + u
            sources = own_wide[pl.ds(k, 2 * boxes, stride=kdir), :].astype(BF16)
            out_ref[pl.ds(k, 2 * boxes, stride=kdir), :] = dot(operator(k)[:, : 2 * boxes], sources)
        return carry

    lax.fori_loop(0, kdir // unroll, near_own, 0)

    for depth in range(2, len(later)):
        for chain in range(2):
            halve(chain, depth)
    for depth in range(len(later), 1, -1):
        for chain in range(2):
            double(chain, depth)

    def land(i, carry):
        back_copy(i).wait()
        return carry

    lax.fori_loop(1, n, land, 0)

    for parent_at in range(groups8):
        for child in range(8):
            b = parent_at * 8 + child
            re = returned[0, parent_at].astype(F32)
            im = returned[1, parent_at].astype(F32)
            cosine = phase_ref[:, child : child + 1]
            sine = phase_ref[:, 8 + child : 9 + child]
            real = (cosine * re + sine * im).astype(BF16)
            imag = (cosine * im - sine * re).astype(BF16)
            both = dot(interp_ref[...], jnp.concatenate([real, imag], axis=1))
            spots = pl.ds(b * kdir, kdir)
            out_ref[spots, :] = out_ref[spots, :] + both[:, :illums]
            spots = pl.ds((boxes + b) * kdir, kdir)
            out_ref[spots, :] = out_ref[spots, :] + both[:, illums:]

    for chain in range(2):
        double(chain, 1)

    def near_half(part, at):
        def widen_far(j, carry):
            far_wide[pl.ds(pl.multiple_of(j * kdir, kdir), kdir), :] = far[part * half + j].astype(F32)
            return carry

        lax.fori_loop(0, half, widen_far, 0)

        def near_far(t, carry):
            for u in range(unroll):
                k = t * unroll + u
                sources = far_wide[pl.ds(k, half, stride=kdir), :].astype(BF16)
                spots = pl.ds(k, 2 * boxes, stride=kdir)
                out_ref[spots, :] = out_ref[spots, :] + dot(operator(k)[:, at : at + half], sources)
            return carry

        lax.fori_loop(0, kdir // unroll, near_far, 0)

    near_half(me % 2, 2 * boxes)
    for chain in range(2):
        doubling(chain, 0).wait()
    near_half(1 - me % 2, 2 * boxes + half)


def shards(
    patterns,
    owner_block,
    low_index,
    low_mask,
    low_table,
    interp,
    shift_angle,
    par_source,
    par_index,
    par_mask,
    par_table,
):
    boxes, kdir, illums = patterns.shape[1:]
    groups8 = boxes // 8
    qdir = interp.shape[1]
    n = lax.axis_size("box")
    listed = owner_block.shape[0]
    parents = par_source.shape[0]
    qloc = qdir // n
    rows = 2 * listed * 8
    sources = low_index.shape[1]

    code = jnp.where(low_mask > 0, low_index, -1)
    own, listed_code = code[:, :boxes], code[:, boxes:]
    spare = jnp.full((boxes, -2 * sources % 128), -1, jnp.int32)
    code = jnp.concatenate([own, own, listed_code, listed_code, spare], axis=1)
    low = jnp.transpose(low_table, (0, 2, 1)).reshape(2 * kdir, -1)
    start = lax.axis_index("box") * qloc
    table = lax.dynamic_slice_in_dim(par_table, start, qloc, 2)
    table = jnp.transpose(table, (0, 2, 1)).reshape(2 * qloc, -1)

    phase = jnp.concatenate([jnp.cos(shift_angle), jnp.sin(shift_angle)], axis=0).T

    vmem = pl.BlockSpec(memory_space=pltpu.VMEM)
    smem = pl.BlockSpec(memory_space=pltpu.SMEM)
    stages = n.bit_length() - 1
    dma = pltpu.SemaphoreType.DMA
    return pl.pallas_call(
        functools.partial(kernel, n, listed),
        out_shape=jax.ShapeDtypeStruct((2 * boxes * kdir, illums), F32),
        in_specs=[smem] + [vmem] * 9,
        out_specs=vmem,
        scratch_shapes=[
            pltpu.VMEM((kdir * 2 * boxes, code.shape[1]), F32),
            pltpu.VMEM((qloc * 2 * parents, 2 * parents), F32),
            pltpu.VMEM((2 * groups8, qdir, illums), BF16),
            pltpu.VMEM((n, 2 * groups8, qloc, illums), BF16),
            pltpu.VMEM((2 * parents * qloc, illums), F32),
            pltpu.VMEM((2 * parents * qloc, illums), F32),
            pltpu.VMEM((2, parents, qloc, illums), BF16),
            pltpu.VMEM((2, groups8, qdir, illums), BF16),
            pltpu.VMEM((rows, kdir, illums), BF16),
            pltpu.VMEM((rows, kdir, illums), BF16),
            pltpu.VMEM((rows, kdir, illums), BF16),
            pltpu.VMEM((rows // 2 * kdir, illums), F32),
            pltpu.VMEM((2 * boxes * kdir, illums), F32),
            dma((n,)),
            dma((n,)),
            dma((n,)),
            dma((n,)),
            dma((2, stages)),
            dma((2, stages)),
            dma((2, stages)),
            dma((2, stages)),
        ],
        compiler_params=pltpu.CompilerParams(
            collective_id=0, has_side_effects=True, vmem_limit_bytes=56 * 1024 * 1024
        ),
    )(
        owner_block,
        patterns,
        code,
        low,
        par_source,
        par_index,
        par_mask,
        table,
        interp,
        phase,
    ).reshape(2, boxes, kdir, illums)


def solution(mesh):
    placed = (
        P(None, "box", None, "illum"),
        P(),
        P("box", None),
        P("box", None),
        P(),
        P(),
        P(),
        P(),
        P(),
        P(),
        P(),
    )
    return jax.shard_map(
        shards, mesh=mesh, in_specs=placed, out_specs=P(None, "box", None, "illum"), check_vma=False
    )
```

```python
import functools

import jax
import jax.numpy as jnp
from jax import lax
from jax.experimental import pallas as pl
from jax.experimental.pallas import tpu as pltpu
from jax.sharding import PartitionSpec as P

F32 = jnp.float32
BF16 = jnp.bfloat16
MESH = pl.DeviceIdType.MESH


def dot(left, right):
    return jnp.dot(left, right, preferred_element_type=F32)


def kernel(
    n,
    listed,
    pitches,
    owner_ref,
    pat_ref,
    code_ref,
    table_ref,
    source_ref,
    index_ref,
    mask_ref,
    par_ref,
    interp_ref,
    angle_ref,
    out_ref,
    phase_ref,
    op,
    couple,
    parent,
    arrived,
    wide,
    result,
    result_send,
    returned,
    buf,
    landed,
    far,
    far_wide,
    own_wide,
    acc,
    out_send,
    out_recv,
    back_send,
    back_recv,
    rs_send,
    rs_recv,
    ag_send,
    ag_recv,
):
    me = lax.axis_index("box")
    boxes = pat_ref.shape[1]
    kdir, illums = pat_ref.shape[2], pat_ref.shape[3]
    groups8 = boxes // 8
    qdir = interp_ref.shape[1]
    qloc = qdir // n
    rows = 2 * listed * 8
    stages = n.bit_length() - 1
    kpitch, bpitch, qpitch, ppitch = pitches

    barrier = pltpu.get_barrier_semaphore()

    def greet(i, carry):
        peer = lax.rem(me + i, n)
        pl.semaphore_signal(barrier, inc=1, device_id={"box": peer}, device_id_type=MESH)
        return carry

    lax.fori_loop(1, n, greet, 0)

    for step in range(listed):
        owner = owner_ref[step]
        mine = owner // groups8 == me
        first = owner % groups8 * 8
        for part in range(2):
            block = pat_ref[part, pl.ds(first, 8)]
            buf[pl.ds((part * listed + step) * 8, 8)] = jnp.where(mine, block, jnp.zeros_like(block))

    pl.semaphore_wait(barrier, n - 1)

    half = rows // 2
    later = list(range(1, stages))
    cut = (stages + 1) // 2
    chains = [later, [b for b in later if b >= cut] + [b for b in later if b < cut]]

    def place(chain, depth):
        low = me % 2 * half + chain * (half // 2)
        size = half // 2
        for b in chains[chain][:depth]:
            size = size // 2
            low = low + me // (1 << b) % 2 * size
        return low, size

    def remote(src, dst, send, recv, bit):
        mine = me // (1 << bit) % 2
        return pltpu.make_async_remote_copy(
            src_ref=src,
            dst_ref=dst,
            send_sem=send,
            recv_sem=recv,
            device_id={"box": me + (1 - 2 * mine) * (1 << bit)},
            device_id_type=MESH,
        )

    def first_swap():
        give = (1 - me % 2) * half
        return remote(
            buf.at[pl.ds(give, half)], landed.at[pl.ds(0, half)], rs_send.at[0, 0], rs_recv.at[0, 0], 0
        )

    def halving(chain, depth):
        bit = chains[chain][depth]
        low, size = place(chain, depth)
        size = size // 2
        give = low + (1 - me // (1 << bit) % 2) * size
        spot = half + chain * (half // 2) + half // 2 - 2 * size
        return remote(
            buf.at[pl.ds(give, size)],
            landed.at[pl.ds(spot, size)],
            rs_send.at[chain, 1 + depth],
            rs_recv.at[chain, 1 + depth],
            bit,
        )

    def halve(chain, depth):
        halving(chain, depth).wait()
        low, size = place(chain, depth + 1)
        spot = half + chain * (half // 2) + half // 2 - 2 * size
        target = far if depth + 1 == len(later) else buf
        target[pl.ds(low, size)] = buf[pl.ds(low, size)] + landed[pl.ds(spot, size)]
        if depth + 1 < len(later):
            halving(chain, depth + 1).start()
        else:
            doubling(chain, len(later)).start()

    def doubling(chain, depth):
        low, size = place(chain, depth)
        bit = chains[chain][depth - 1] if depth else 0
        spots = far.at[pl.ds(low, size)]
        return remote(spots, spots, ag_send.at[chain, depth], ag_recv.at[chain, depth], bit)

    def double(chain, depth):
        doubling(chain, depth).wait()
        doubling(chain, depth - 1).start()

    first_swap().start()
    phase_ref[:, :8] = jnp.cos(angle_ref[...]).T
    phase_ref[:, 8:] = jnp.sin(angle_ref[...]).T

    tile = 256
    for parent_at in range(groups8):

        def lift(t, carry, parent_at=parent_at):
            at = pl.multiple_of(t * tile, tile)
            left = interp_ref[:, pl.ds(at, tile)].T
            real = jnp.zeros((tile, illums), F32)
            imag = jnp.zeros((tile, illums), F32)
            for child in range(8):
                b = parent_at * 8 + child
                both = dot(left, jnp.concatenate([pat_ref[0, b], pat_ref[1, b]], axis=1))
                cosine = phase_ref[pl.ds(at, tile), child : child + 1]
                sine = phase_ref[pl.ds(at, tile), 8 + child : 9 + child]
                re, im = both[:, :illums], both[:, illums:]
                real = real + (cosine * re - sine * im)
                imag = imag + (cosine * im + sine * re)
            parent[parent_at, pl.ds(at, tile), :] = real.astype(BF16)
            parent[groups8 + parent_at, pl.ds(at, tile), :] = imag.astype(BF16)
            return carry

        lax.fori_loop(0, qdir // tile, lift, 0)

    def out_copy(i):
        peer = lax.rem(me + i, n)
        return pltpu.make_async_remote_copy(
            src_ref=parent.at[:, pl.ds(pl.multiple_of(peer * qloc, qloc), qloc), :],
            dst_ref=arrived.at[me],
            send_sem=out_send.at[i],
            recv_sem=out_recv.at[i],
            device_id={"box": peer},
            device_id_type=MESH,
        )

    def start_out(i, carry):
        out_copy(i).start()
        return carry

    lax.fori_loop(1, n, start_out, 0)

    first_swap().wait()
    kept = pl.ds(me % 2 * half, half)
    buf[kept] = buf[kept] + landed[pl.ds(0, half)]
    halving(0, 0).start()
    halving(1, 0).start()

    unroll = 8
    parents = n * groups8
    parents2 = 2 * parents

    lanes = lax.broadcasted_iota(jnp.int32, (parents, parents), 1)
    code = jnp.zeros((parents, parents), jnp.int32)
    slot_code = jnp.where(mask_ref[...] > 0, index_ref[...] + 1, 0).T
    slot_source = source_ref[...].T
    for j in range(source_ref.shape[0]):
        code = code + jnp.where(slot_source[:, j : j + 1] == lanes, slot_code[:, j : j + 1], 0)
    code = jnp.concatenate([code, code], axis=1) - 1
    each = max(1, 256 // parents2)
    kinds = lax.broadcasted_iota(jnp.int32, (par_ref.shape[1], each * parents2), 0)
    first = lax.broadcasted_iota(jnp.int32, (qloc, parents2), 1) < parents
    for p in range(0, parents, each):
        row = jnp.concatenate([code[p + u : p + u + 1] for u in range(each)], axis=1)
        hot = jnp.where(kinds == row, 1.0, 0.0).astype(BF16)
        got = dot(par_ref[...], hot)
        for u in range(each):
            real = got[:qloc, u * parents2 : (u + 1) * parents2]
            imag = got[qloc:, u * parents2 : (u + 1) * parents2]
            couple[pl.ds(p + u, qloc, stride=ppitch), :] = jnp.where(first, real, -imag)
            couple[pl.ds(parents + p + u, qloc, stride=ppitch), :] = jnp.where(first, imag, real)

    width = code_ref.shape[1]
    low_kinds = lax.broadcasted_iota(jnp.int32, (table_ref.shape[1], 2 * width), 0)
    lane = lax.broadcasted_iota(jnp.int32, (kdir, width), 1)
    flip = me % 2
    column = jnp.where(
        lane < 2 * boxes, lane // boxes, jnp.where(lane < 2 * boxes + half, flip, 1 - flip)
    )
    low_first = column == 0
    for b in range(0, boxes, 2):
        row = jnp.concatenate([code_ref[b : b + 1], code_ref[b + 1 : b + 2]], axis=1)
        hot = jnp.where(low_kinds == row, 1.0, 0.0).astype(BF16)
        got = dot(table_ref[...], hot)
        for u in range(2):
            real = got[:kdir, u * width : (u + 1) * width]
            imag = got[kdir:, u * width : (u + 1) * width]
            op[pl.ds(b + u, kdir, stride=bpitch), :] = jnp.where(low_first, real, -imag)
            op[pl.ds(boxes + b + u, kdir, stride=bpitch), :] = jnp.where(low_first, imag, real)

    def operator(k):
        return op[pl.ds(pl.multiple_of(k * bpitch, 8), 2 * boxes), :].astype(BF16)

    for chain in range(2):
        halve(chain, 0)

    def widen(source, value):
        for part in range(2):
            for p in range(groups8):
                s = (part * n + source) * groups8 + p
                at = pl.multiple_of(s * qpitch, 8)
                wide[pl.ds(at, qloc), :] = value(part * groups8 + p).astype(F32)

    widen(me, lambda c: parent[c, pl.ds(pl.multiple_of(me * qloc, qloc), qloc), :])

    def take(i, carry):
        out_copy(i).wait()
        source = lax.rem(me - i + n, n)
        widen(source, lambda c: arrived[source, c])
        return carry

    lax.fori_loop(1, n, take, 0)
    def translate(t, carry):
        for u in range(unroll):
            q = t * unroll + u
            sources = wide[pl.ds(q, parents2, stride=qpitch), :].astype(BF16)
            result[pl.ds(q, parents2, stride=qpitch), :] = dot(
                couple[pl.ds(pl.multiple_of(q * ppitch, 8), parents2), :].astype(BF16), sources
            )
        return carry

    lax.fori_loop(0, qloc // unroll, translate, 0)
    for s in range(parents2):
        result_send[s // parents, s % parents] = result[pl.ds(s * qpitch, qloc), :].astype(BF16)

    def back_copy(i):
        peer = lax.rem(me + i, n)
        return pltpu.make_async_remote_copy(
            src_ref=result_send.at[:, pl.ds(peer * groups8, groups8)],
            dst_ref=returned.at[:, :, pl.ds(pl.multiple_of(me * qloc, qloc), qloc), :],
            send_sem=back_send.at[i],
            recv_sem=back_recv.at[i],
            device_id={"box": peer},
            device_id_type=MESH,
        )

    def start_back(i, carry):
        back_copy(i).start()
        return carry

    lax.fori_loop(1, n, start_back, 0)
    returned[:, :, pl.ds(pl.multiple_of(me * qloc, qloc), qloc), :] = result_send[:, pl.ds(me * groups8, groups8)]

    for chain in range(2):
        halve(chain, 1)

    for part in range(2):
        for b in range(boxes):
            own_wide[pl.ds((part * boxes + b) * kpitch, kdir), :] = pat_ref[part, b].astype(F32)

    def near_own(t, carry):
        sums = []
        for u in range(unroll):
            k = t * unroll + u
            sources = own_wide[pl.ds(k, 2 * boxes, stride=kpitch), :].astype(BF16)
            sums.append(dot(operator(k)[:, : 2 * boxes], sources))
        for u in range(unroll):
            acc[pl.ds(t * unroll + u, 2 * boxes, stride=kpitch), :] = sums[u]
        return carry

    lax.fori_loop(0, kdir // unroll, near_own, 0)

    for depth in range(2, len(later)):
        for chain in range(2):
            halve(chain, depth)
    for depth in range(len(later), 1, -1):
        for chain in range(2):
            double(chain, depth)

    def land(i, carry):
        back_copy(i).wait()
        return carry

    lax.fori_loop(1, n, land, 0)

    for parent_at in range(groups8):
        for child in range(8):
            b = parent_at * 8 + child
            re = returned[0, parent_at].astype(F32)
            im = returned[1, parent_at].astype(F32)
            cosine = phase_ref[:, child : child + 1]
            sine = phase_ref[:, 8 + child : 9 + child]
            real = (cosine * re + sine * im).astype(BF16)
            imag = (cosine * im - sine * re).astype(BF16)
            both = dot(interp_ref[...], jnp.concatenate([real, imag], axis=1))
            spots = pl.ds(b * kdir, kdir)
            out_ref[spots, :] = both[:, :illums]
            spots = pl.ds((boxes + b) * kdir, kdir)
            out_ref[spots, :] = both[:, illums:]

    for chain in range(2):
        double(chain, 1)

    def near_half(part, at):
        def widen_far(j, carry):
            far_wide[pl.ds(pl.multiple_of(j * kpitch, 8), kdir), :] = far[part * half + j].astype(F32)
            return carry

        lax.fori_loop(0, half, widen_far, 0)

        def near_far(t, carry):
            sums = []
            for u in range(unroll):
                k = t * unroll + u
                sources = far_wide[pl.ds(k, half, stride=kpitch), :].astype(BF16)
                spots = pl.ds(k, 2 * boxes, stride=kpitch)
                sums.append(acc[spots, :] + dot(operator(k)[:, at : at + half], sources))
            for u in range(unroll):
                acc[pl.ds(t * unroll + u, 2 * boxes, stride=kpitch), :] = sums[u]
            return carry

        lax.fori_loop(0, kdir // unroll, near_far, 0)

    near_half(me % 2, 2 * boxes)
    for chain in range(2):
        doubling(chain, 0).wait()
    near_half(1 - me % 2, 2 * boxes + half)

    for b in range(2 * boxes):
        spots = pl.ds(b * kdir, kdir)
        out_ref[spots, :] = out_ref[spots, :] + acc[pl.ds(b * kpitch, kdir), :]


def shards(
    patterns,
    owner_block,
    low_index,
    low_mask,
    low_table,
    interp,
    shift_angle,
    par_source,
    par_index,
    par_mask,
    par_table,
):
    boxes, kdir, illums = patterns.shape[1:]
    groups8 = boxes // 8
    qdir = interp.shape[1]
    n = lax.axis_size("box")
    listed = owner_block.shape[0]
    parents = par_source.shape[0]
    qloc = qdir // n
    rows = 2 * listed * 8
    sources = low_index.shape[1]

    code = jnp.where(low_mask > 0, low_index, -1)
    own, listed_code = code[:, :boxes], code[:, boxes:]
    spare = jnp.full((boxes, -2 * sources % 128), -1, jnp.int32)
    code = jnp.concatenate([own, own, listed_code, listed_code, spare], axis=1)
    low = jnp.transpose(low_table, (0, 2, 1)).reshape(2 * kdir, -1)
    start = lax.axis_index("box") * qloc
    table = lax.dynamic_slice_in_dim(par_table, start, qloc, 2)
    table = jnp.transpose(table, (0, 2, 1)).reshape(2 * qloc, -1)

    pitches = (kdir + 8, 2 * boxes + 8, qloc + 8, 2 * parents + 8)
    kpitch, bpitch, qpitch, ppitch = pitches
    vmem = pl.BlockSpec(memory_space=pltpu.VMEM)
    smem = pl.BlockSpec(memory_space=pltpu.SMEM)
    stages = n.bit_length() - 1
    dma = pltpu.SemaphoreType.DMA
    return pl.pallas_call(
        functools.partial(kernel, n, listed, pitches),
        out_shape=jax.ShapeDtypeStruct((2 * boxes * kdir, illums), F32),
        in_specs=[smem] + [vmem] * 9,
        out_specs=vmem,
        scratch_shapes=[
            pltpu.VMEM((qdir, 16), F32),
            pltpu.VMEM((kdir * bpitch, code.shape[1]), F32),
            pltpu.VMEM((qloc * ppitch, 2 * parents), F32),
            pltpu.VMEM((2 * groups8, qdir, illums), BF16),
            pltpu.VMEM((n, 2 * groups8, qloc, illums), BF16),
            pltpu.VMEM((2 * parents * qpitch, illums), F32),
            pltpu.VMEM((2 * parents * qpitch, illums), F32),
            pltpu.VMEM((2, parents, qloc, illums), BF16),
            pltpu.VMEM((2, groups8, qdir, illums), BF16),
            pltpu.VMEM((rows, kdir, illums), BF16),
            pltpu.VMEM((rows, kdir, illums), BF16),
            pltpu.VMEM((rows, kdir, illums), BF16),
            pltpu.VMEM((rows // 2 * kpitch, illums), F32),
            pltpu.VMEM((2 * boxes * kpitch, illums), F32),
            pltpu.VMEM((2 * boxes * kpitch, illums), F32),
            dma((n,)),
            dma((n,)),
            dma((n,)),
            dma((n,)),
            dma((2, stages)),
            dma((2, stages)),
            dma((2, stages)),
            dma((2, stages)),
        ],
        compiler_params=pltpu.CompilerParams(
            collective_id=0, has_side_effects=True, vmem_limit_bytes=56 * 1024 * 1024
        ),
    )(
        owner_block,
        patterns,
        code,
        low,
        par_source.T,
        par_index.T,
        par_mask.T,
        table,
        interp,
        shift_angle,
    ).reshape(2, boxes, kdir, illums)


def solution(mesh):
    placed = (
        P(None, "box", None, "illum"),
        P(),
        P("box", None),
        P("box", None),
        P(),
        P(),
        P(),
        P(),
        P(),
        P(),
        P(),
    )
    return jax.shard_map(
        shards, mesh=mesh, in_specs=placed, out_specs=P(None, "box", None, "illum"), check_vma=False
    )
```
